32 devices in a mesh: dom: 4 (over y, core), work: 8 (over z, x).
Axes of the slice: x: 2, y: 2, z: 4, core: 2. Of those that a mesh axis runs over, the one named last changes fastest.
Arguments:
- entity: float32 [4096, 400], P(('dom', 'work')), may hold values from -1.2 to 1.2
- row_state: float32 [4096], P(('dom', 'work')), may hold values from 0.001 to 0.03
- relation_table: bfloat16 [4096, 400], replicated, may hold values from -6 to 6
- edge_heads: int32 [16384], P(('dom', 'work')), may hold values from 0 to 1023, as said below
- edge_relations: int32 [16384], P(('dom', 'work')), may hold values from 0 to 4095
- edge_tails: int32 [16384], P(('dom', 'work')), may hold values from 0 to 1023, as said below
- plan: int32 [4], replicated, may hold values from 0 to 3, as said below
- negative_start: int32 [4], replicated, may hold values from 0 to 1023
Outputs:
- entity_new: float32 [4096, 400], P(('dom', 'work'))
- state_new: float32 [4096], P(('dom', 'work'))
The draws below stay inside these ranges and needn't reach their ends.
Inputs may be any that keep to these rules, and one draw needn't show every extreme that they name: plan is a permutation of the groups. `edge_heads`: the edges held by worker w of a group have heads in rows w * 128 to (w + 1) * 128 - 1 of the group's partition. `edge_tails`: of the edges of one device at most 80 have tails in rows w * 128 to (w + 1) * 128 - 1 for any w, and on every device some w has exactly 80.
All inputs are finite; a program needn't handle non-finite values.
Results may differ from the reference program's by a relative error of at most 0.0003.
The reference program's roundings to bfloat16 on the way (of `table`, `head_rows`, `queries`, `negatives` and `weights`) count: a program that leaves them out, or rounds other values in their place, can miss the bound.
Values may be sent and summed in bfloat16 or wider, within the bound.
A program may use at most 64 MiB of HBM per device.

```python
import math
import jax
import jax.numpy as jnp
from jax import lax

D = 400
RELS = 4096
NEG = 1024
ENT_DEV = 128
EDGE_DEV = 512
CAP = 80
ENT_PART = 1024
ENTITIES = 4096
EDGES = 16384
N_DOM = 4
N_WORK = 8


def tail_block(key):
    workers = ENT_PART // ENT_DEV
    key_owner, key_mix, key_order, key_row = jax.random.split(key, 4)
    full_owner = jax.random.randint(key_owner, (), 0, workers, dtype=jnp.int32)
    owner_pool = jnp.repeat(jnp.arange(workers, dtype=jnp.int32), CAP)
    mixed = jax.random.permutation(key_mix, owner_pool)
    ordering = jnp.argsort(jnp.where(mixed == full_owner, 0, 1), stable=True)
    chosen = jax.random.permutation(key_order, mixed[ordering][:EDGE_DEV])
    local_rows = jax.random.randint(key_row, (EDGE_DEV,), 0, ENT_DEV, dtype=jnp.int32)
    return chosen * ENT_DEV + local_rows


def draw_edge_tails(key, part):
    blocks = EDGES // EDGE_DEV
    block_keys = jax.random.split(jax.random.fold_in(key, 7), blocks)
    return jax.vmap(tail_block)(block_keys).reshape(-1).astype(jnp.int32)


def draw_edge_heads(key, part):
    blocks = EDGES // EDGE_DEV
    workers = ENT_PART // ENT_DEV
    owner_of = (jnp.arange(blocks, dtype=jnp.int32) % workers)[:, None]
    local_rows = jax.random.randint(jax.random.fold_in(key, 3), (blocks, EDGE_DEV), 0, ENT_DEV, dtype=jnp.int32)
    return (owner_of * ENT_DEV + local_rows).reshape(-1).astype(jnp.int32)


def draw_plan(key, part):
    domains = ENTITIES // ENT_PART
    key_perm, key_pick = jax.random.split(jax.random.fold_in(key, 5), 2)
    shuffled = jax.random.permutation(key_perm, jnp.arange(domains, dtype=jnp.int32))
    picked = jax.random.randint(key_pick, (), 0, domains, dtype=jnp.int32)
    far_part = (picked + domains // 2) % domains
    where_far = jnp.argmax((shuffled == far_part).astype(jnp.int32)).astype(jnp.int32)
    moved = shuffled.at[where_far].set(shuffled[picked])
    return moved.at[picked].set(far_part).astype(jnp.int32)


def with_ends(array, rng, least, high):
    longest = array.shape.index(max(array.shape))
    spots = []
    for shift in (0, 1):
        where = [jax.random.randint(jax.random.fold_in(rng, axis), (), 0, length) for axis, length in enumerate(array.shape)]
        where[longest] = (where[longest] + shift) % array.shape[longest]
        spots.append(tuple(where))
    return array.at[spots[0]].set(least).at[spots[1]].set(high)


def levels(rng, extent, pieces, least, high):
    level = 1.0
    for position, parts in pieces:
        draws = jax.random.uniform(jax.random.fold_in(jax.random.fold_in(rng, 6), position), (parts,), jnp.float32, least / len(pieces), high / len(pieces))
        level = level * jnp.repeat(jnp.exp(draws), extent[position] // parts).reshape((-1,) + (1,) * (len(extent) - 1 - position))
    return level


def noise(key, dims, scale, limit, shards=(), kind=jnp.bfloat16):
    result = scale * jax.random.normal(key, dims, jnp.float32)
    if shards:
        result = result * levels(key, dims, shards, -0.22, 0.18)
    return jnp.clip(result, -limit, limit).astype(kind)


def setup_inputs(seed: int = 0) -> dict:
    splits = jax.random.split(jax.random.key(seed), 9)
    entity = noise(splits[0], (ENTITIES, D), 0.2, 1.2, ((0, 32),), jnp.float32)
    row_state = jnp.clip(jnp.exp(math.log(0.03) - 3.4011973 * jax.random.uniform(splits[1], (ENTITIES,), jnp.float32) ** levels(splits[1], (ENTITIES,), ((0, 32),), -0.2, 0.2)), 0.001, 0.03)
    relation_table = noise(splits[2], (RELS, D), 1.0, 6.0)
    edge_heads = draw_edge_heads(jax.random.fold_in(splits[8], 71), 0)
    edge_relations = with_ends(jax.random.randint(splits[4], (EDGES,), 0, RELS), jax.random.fold_in(splits[4], 1), 0, RELS - 1).astype(jnp.int32)
    edge_tails = draw_edge_tails(jax.random.fold_in(splits[8], 71), 0)
    plan = draw_plan(jax.random.fold_in(splits[8], 71), 0)
    negative_start = with_ends(jax.random.randint(splits[7], (N_DOM,), 0, ENT_PART), jax.random.fold_in(splits[7], 1), 0, ENT_PART - 1).astype(jnp.int32)
    return {"entity": entity, "row_state": row_state, "relation_table": relation_table, "edge_heads": edge_heads, "edge_relations": edge_relations, "edge_tails": edge_tails, "plan": plan, "negative_start": negative_start}


learn_rate = 0.1

def complex_query(head_rows, rel_rows):
    half_width = head_rows.shape[-1] // 2
    head_float = head_rows.astype(jnp.float32)
    relation = rel_rows.astype(jnp.float32)
    head_real, head_imaginary = (head_float[:, :half_width], head_float[:, half_width:])
    relation_real, relation_imaginary = (relation[:, :half_width], relation[:, half_width:])
    first = head_real * relation_real - head_imaginary * relation_imaginary
    second = head_real * relation_imaginary + head_imaginary * relation_real
    return jnp.concatenate([first, second], axis=1).astype(jnp.bfloat16)

def head_gradient(query_grad, rel_rows):
    half_width = query_grad.shape[-1] // 2
    relation = rel_rows.astype(jnp.float32)
    grad_real, grad_imaginary = (query_grad[:, :half_width], query_grad[:, half_width:])
    relation_real, relation_imaginary = (relation[:, :half_width], relation[:, half_width:])
    first = grad_real * relation_real + grad_imaginary * relation_imaginary
    second = grad_imaginary * relation_real - grad_real * relation_imaginary
    return jnp.concatenate([first, second], axis=1)

def negative_pass(queries, negatives, block_rows):
    edge_count, features = queries.shape
    num_blocks = edge_count // block_rows
    stacked = queries.reshape(num_blocks, block_rows, features)
    factor = 1.0 / math.sqrt(negatives.shape[0])

    def one_block(negative_grad, block_queries):
        scores = jnp.dot(block_queries, negatives.T, preferred_element_type=jnp.float32)
        weights = (jax.nn.sigmoid(scores) * factor).astype(jnp.bfloat16)
        pulled = jnp.dot(weights, negatives, preferred_element_type=jnp.float32)
        negative_grad = negative_grad + jnp.dot(weights.T, block_queries, preferred_element_type=jnp.float32)
        return (negative_grad, pulled)
    zero_grad = jnp.zeros((negatives.shape[0], features), jnp.float32)
    negative_grad, pulled = lax.scan(one_block, zero_grad, stacked)
    return (pulled.reshape(edge_count, features), negative_grad)

def reference(entity, row_state, relation_table, edge_heads, edge_relations, edge_tails, plan, negative_start):
    part_rows = ENT_DEV * N_WORK
    group_edges = EDGE_DEV * N_WORK
    table = entity.astype(jnp.bfloat16)
    gradient = jnp.zeros(entity.shape, jnp.float32)
    for domain_index in range(N_DOM):
        target = plan[domain_index]
        source_part = table[domain_index * part_rows:(domain_index + 1) * part_rows]
        target_part = lax.dynamic_slice_in_dim(table, (target * part_rows).astype(jnp.int32), part_rows, 0)
        first_edge = domain_index * group_edges
        head_index = edge_heads[first_edge:first_edge + group_edges]
        relation_index = edge_relations[first_edge:first_edge + group_edges]
        tail_index = edge_tails[first_edge:first_edge + group_edges]
        head_rows = source_part[head_index]
        tail_rows = target_part[tail_index]
        rel_rows = relation_table[relation_index]
        queries = complex_query(head_rows, rel_rows)
        negative_rows = ((negative_start[domain_index] + jnp.arange(NEG, dtype=jnp.int32)) % part_rows).astype(jnp.int32)
        negatives = target_part[negative_rows]
        positive = lax.optimization_barrier(jnp.sum(queries.astype(jnp.float32) * tail_rows.astype(jnp.float32), axis=1))
        positive_weight = jax.nn.sigmoid(positive) - 1.0
        pulled, negative_grad = negative_pass(queries, negatives, min(512, group_edges))
        query_grad = positive_weight[:, None] * tail_rows.astype(jnp.float32) + pulled
        gradient = gradient.at[domain_index * part_rows + head_index].add(head_gradient(query_grad, rel_rows))
        gradient = gradient.at[target * part_rows + tail_index].add(positive_weight[:, None] * queries.astype(jnp.float32))
        gradient = gradient.at[target * part_rows + negative_rows].add(negative_grad)
    state_new = row_state + lax.optimization_barrier(jnp.mean(gradient * gradient, axis=1))
    entity_new = entity - learn_rate * gradient / jnp.sqrt(state_new)[:, None]
    return (entity_new, state_new)
```

```python
import functools
import math

import jax
import jax.numpy as jnp
from jax import lax
from jax.experimental import pallas as pl
from jax.experimental.pallas import tpu as pltpu
from jax.sharding import PartitionSpec as P

NEG = 1024
learn_rate = 0.1
MESH = pl.DeviceIdType.MESH
F32 = jnp.float32
BF16 = jnp.bfloat16
GRAD = F32


def dot_nn(a, b):
    return lax.dot_general(a, b, (((1,), (0,)), ((), ())), preferred_element_type=F32)


def dot_nt(a, b):
    return lax.dot_general(a, b, (((1,), (1,)), ((), ())), preferred_element_type=F32)


def split(value):
    high = value.astype(BF16)
    low = (value - high.astype(F32)).astype(BF16)
    return high, low


def transpose_pad(value):
    n, m = value.shape
    pad = -m % 128
    if pad:
        value = jnp.concatenate([value, jnp.zeros((n, pad), value.dtype)], axis=1)
    return jnp.transpose(value)[:m]


def untranspose_pad(value):
    m, n = value.shape
    pad = -m % 128
    if pad:
        value = jnp.concatenate([value, jnp.zeros((pad, n), value.dtype)], axis=0)
    return jnp.transpose(value)[:, :m]


def kernel(
    domains,
    workers,
    entity_ref,
    state_ref,
    relation_hbm,
    heads_ref,
    relations_ref,
    tails_ref,
    plan_ref,
    start_ref,
    entity_out,
    state_out,
    relation_vmem,
    parts,
    target_part,
    partial,
    summed,
    returned,
    rel_rows,
    pulled,
    query_t,
    query_e,
    tail_hi,
    tail_lo,
    relation_sem,
    parts_send,
    parts_recv,
    target_send,
    target_recv,
    sum_send,
    sum_recv,
    return_send,
    return_recv,
):
    rows, features = entity_ref.shape
    half = features // 2
    edges = heads_ref.shape[1]
    relations = relation_hbm.shape[0]
    part_rows = rows * workers
    dom = lax.axis_index("dom")
    me = lax.axis_index("work")

    relation_copy = pltpu.make_async_copy(relation_hbm, relation_vmem, relation_sem)
    relation_copy.start()

    barrier = pltpu.get_barrier_semaphore()

    def dom_peer(k):
        return lax.rem(dom + k, domains)

    def work_peer(k):
        return lax.rem(me + k, workers)

    def from_dom(k):
        return lax.rem(dom + domains - k, domains)

    def from_work(k):
        return lax.rem(me + workers - k, workers)

    for k in range(1, domains):
        pl.semaphore_signal(barrier, inc=1, device_id=(dom_peer(k), me), device_id_type=MESH)
    for k in range(1, workers):
        pl.semaphore_signal(barrier, inc=1, device_id=(dom, work_peer(k)), device_id_type=MESH)

    entity_t = transpose_pad(entity_ref[...])
    table_t = entity_t.astype(BF16)
    parts[dom] = table_t
    pl.semaphore_wait(barrier, domains + workers - 2)

    def parts_copy(k):
        return pltpu.make_async_remote_copy(
            src_ref=parts.at[dom],
            dst_ref=parts.at[dom],
            send_sem=parts_send.at[k],
            recv_sem=parts_recv.at[k],
            device_id=(dom_peer(k), me),
            device_id_type=MESH,
        )

    def parts_arrival(k):
        return pltpu.make_async_remote_copy(
            src_ref=parts.at[from_dom(k)],
            dst_ref=parts.at[from_dom(k)],
            send_sem=parts_send.at[k],
            recv_sem=parts_recv.at[k],
            device_id=(dom_peer(k), me),
            device_id_type=MESH,
        )

    for k in range(1, domains):
        parts_copy(k).start()

    head_local = heads_ref[...] - me * rows
    head_hot = (
        lax.broadcasted_iota(jnp.int32, (rows, edges), 0) == head_local
    ).astype(F32).astype(BF16)
    head_t = dot_nn(table_t, head_hot)

    for k in range(1, domains):
        parts_arrival(k).wait_recv()
    target = plan_ref[dom]
    target_part[me] = parts[target]

    def target_copy(k):
        return pltpu.make_async_remote_copy(
            src_ref=target_part.at[me],
            dst_ref=target_part.at[me],
            send_sem=target_send.at[k],
            recv_sem=target_recv.at[k],
            device_id=(dom, work_peer(k)),
            device_id_type=MESH,
        )

    def target_arrival(k):
        return pltpu.make_async_remote_copy(
            src_ref=target_part.at[from_work(k)],
            dst_ref=target_part.at[from_work(k)],
            send_sem=target_send.at[k],
            recv_sem=target_recv.at[k],
            device_id=(dom, work_peer(k)),
            device_id_type=MESH,
        )

    for k in range(1, workers):
        target_copy(k).start()

    relation_index = jnp.transpose(
        jnp.broadcast_to(relations_ref[...], (128, edges)).astype(F32)
    ).astype(jnp.int32)
    relation_copy.wait()
    rel_rows[...] = jnp.zeros_like(rel_rows)
    step_rows = 512

    def relation_step(step, carry):
        base = pl.multiple_of(step * step_rows, step_rows)
        lane = lax.broadcasted_iota(jnp.int32, (edges, 128), 1)
        hot = jnp.concatenate(
            [
                (relation_index == lane + (base + j * 128)).astype(F32).astype(BF16)
                for j in range(step_rows // 128)
            ],
            axis=1,
        )
        rel_rows[...] += dot_nn(hot, relation_vmem[pl.ds(base, step_rows), :])
        return carry

    lax.fori_loop(0, relations // step_rows, relation_step, 0)
    rel_t = transpose_pad(rel_rows[...])
    rel_x, rel_y = rel_t[:half], rel_t[half:]
    head_x, head_y = head_t[:half], head_t[half:]
    query = jnp.concatenate(
        [head_x * rel_x - head_y * rel_y, head_x * rel_y + head_y * rel_x], axis=0
    )
    query_bf = query.astype(BF16)
    query_t[...] = query_bf
    query_float = query_bf.astype(F32)
    query_e[...] = untranspose_pad(query_float).astype(BF16)

    for k in range(1, workers):
        target_arrival(k).wait_recv()

    def tail_hot(first, count):
        row = lax.broadcasted_iota(jnp.int32, (count, edges), 0) + first
        return (row == tails_ref[...]).astype(F32).astype(BF16)

    pair = 2
    width = pair * rows

    def pair_of(block):
        return jnp.concatenate([target_part[block * pair + j] for j in range(pair)], axis=1)

    pulled[...] = jnp.zeros_like(pulled)

    def tail_step(block, carry):
        pulled[...] += dot_nn(pair_of(block), tail_hot(block * width, width))
        return carry

    lax.fori_loop(0, workers // pair, tail_step, 0)
    tail_t = pulled[...]
    positive = jnp.sum(query_float * tail_t, axis=0, keepdims=True)
    positive_weight = jax.nn.sigmoid(positive) - 1.0
    pulled[...] = positive_weight * tail_t
    high, low = split(positive_weight * query_float)
    tail_hi[...] = high
    tail_lo[...] = low
    factor = 1.0 / math.sqrt(NEG)
    first_negative = start_ref[dom]

    def sum_copy(dest, k):
        return pltpu.make_async_remote_copy(
            src_ref=partial.at[dest],
            dst_ref=summed.at[me],
            send_sem=sum_send.at[dest],
            recv_sem=sum_recv.at[me],
            device_id=(dom, dest),
            device_id_type=MESH,
        )

    def sum_arrival(source):
        return pltpu.make_async_remote_copy(
            src_ref=partial.at[source],
            dst_ref=summed.at[source],
            send_sem=sum_send.at[source],
            recv_sem=sum_recv.at[source],
            device_id=(dom, source),
            device_id_type=MESH,
        )

    def score_step(step, carry):
        block = lax.rem(me // pair + step + 1, workers // pair)
        part = pair_of(block)
        scores = dot_nn(query_e[...], part)
        row = lax.broadcasted_iota(jnp.int32, (1, width), 1) + block * width
        offset = row - first_negative
        offset = jnp.where(offset < 0, offset + part_rows, offset)
        weights = jax.nn.sigmoid(scores) * factor
        if part_rows > NEG:
            weights = jnp.where(offset < NEG, weights, 0.0)
        weights = weights.astype(BF16)
        pulled[...] += dot_nt(part, weights)
        hot = tail_hot(block * width, width)
        grad = (
            dot_nn(query_t[...], weights) + dot_nt(tail_hi[...], hot) + dot_nt(tail_lo[...], hot)
        )
        for j in range(pair):
            dest = block * pair + j
            partial[dest] = grad[:, j * rows : (j + 1) * rows].astype(GRAD)

            @pl.when(dest != me)
            def _():
                sum_copy(dest, 0).start()

        return carry

    lax.fori_loop(0, workers // pair, score_step, 0)

    grad_t = pulled[...]
    grad_x, grad_y = grad_t[:half], grad_t[half:]
    rel_t = transpose_pad(rel_rows[...])
    rel_x, rel_y = rel_t[:half], rel_t[half:]
    head_grad = jnp.concatenate(
        [grad_x * rel_x + grad_y * rel_y, grad_y * rel_x - grad_x * rel_y], axis=0
    )
    high, low = split(head_grad)
    own_grad = dot_nt(high, head_hot) + dot_nt(low, head_hot)

    total = partial[me].astype(F32)
    for k in range(1, workers):
        source = from_work(k)
        sum_arrival(source).wait_recv()
        total = total + summed[source].astype(F32)
    returned[dom] = total.astype(GRAD)

    def return_copy(k):
        return pltpu.make_async_remote_copy(
            src_ref=returned.at[dom],
            dst_ref=returned.at[dom],
            send_sem=return_send.at[k],
            recv_sem=return_recv.at[k],
            device_id=(dom_peer(k), me),
            device_id_type=MESH,
        )

    def return_arrival(k):
        return pltpu.make_async_remote_copy(
            src_ref=returned.at[from_dom(k)],
            dst_ref=returned.at[from_dom(k)],
            send_sem=return_send.at[k],
            recv_sem=return_recv.at[k],
            device_id=(dom_peer(k), me),
            device_id_type=MESH,
        )

    for k in range(1, domains):
        return_copy(k).start()
    giver = jnp.int32(0)
    for p in range(1, domains):
        giver = jnp.where(plan_ref[p] == dom, jnp.int32(p), giver)
    for k in range(1, domains):
        return_arrival(k).wait_recv()
    gradient = own_grad + returned[giver].astype(F32)
    state_new = state_ref[...] + jnp.sum(gradient * gradient, axis=0, keepdims=True) / features
    state_out[...] = state_new
    entity_new = transpose_pad(entity_ref[...]) - learn_rate * gradient / jnp.sqrt(state_new)
    entity_out[...] = untranspose_pad(entity_new)

    for k in range(1, domains):
        parts_copy(k).wait_send()
        return_copy(k).wait_send()
    for k in range(1, workers):
        target_copy(k).wait_send()
        sum_copy(work_peer(k), k).wait_send()


def body(
    domains,
    workers,
    entity,
    row_state,
    relation_table,
    edge_heads,
    edge_relations,
    edge_tails,
    plan,
    negative_start,
):
    rows, features = entity.shape
    edges = edge_heads.shape[0]
    vmem = pl.BlockSpec(memory_space=pltpu.VMEM)
    smem = pl.BlockSpec(memory_space=pltpu.SMEM)
    entity_new, state_new = pl.pallas_call(
        functools.partial(kernel, domains, workers),
        out_shape=(
            jax.ShapeDtypeStruct((rows, features), F32),
            jax.ShapeDtypeStruct((1, rows), F32),
        ),
        in_specs=[vmem, vmem, pl.BlockSpec(memory_space=pl.ANY), vmem, vmem, vmem, smem, smem],
        out_specs=(vmem, vmem),
        scratch_shapes=[
            pltpu.VMEM(relation_table.shape, BF16),
            pltpu.VMEM((domains, features, rows), BF16),
            pltpu.VMEM((workers, features, rows), BF16),
            pltpu.VMEM((workers, features, rows), GRAD),
            pltpu.VMEM((workers, features, rows), GRAD),
            pltpu.VMEM((domains, features, rows), GRAD),
            pltpu.VMEM((edges, features), F32),
            pltpu.VMEM((features, edges), F32),
            pltpu.VMEM((features, edges), BF16),
            pltpu.VMEM((edges, features), BF16),
            pltpu.VMEM((features, edges), BF16),
            pltpu.VMEM((features, edges), BF16),
            pltpu.SemaphoreType.DMA,
            pltpu.SemaphoreType.DMA((domains,)),
            pltpu.SemaphoreType.DMA((domains,)),
            pltpu.SemaphoreType.DMA((workers,)),
            pltpu.SemaphoreType.DMA((workers,)),
            pltpu.SemaphoreType.DMA((workers,)),
            pltpu.SemaphoreType.DMA((workers,)),
            pltpu.SemaphoreType.DMA((domains,)),
            pltpu.SemaphoreType.DMA((domains,)),
        ],
        compiler_params=pltpu.CompilerParams(
            collective_id=0, has_side_effects=True, vmem_limit_bytes=50 << 20
        ),
    )(
        entity,
        row_state.reshape(1, rows),
        relation_table,
        edge_heads.reshape(1, edges),
        edge_relations.reshape(1, edges),
        edge_tails.reshape(1, edges),
        plan,
        negative_start,
    )
    return entity_new, state_new.reshape(rows)


def solution(mesh):
    return jax.shard_map(
        functools.partial(body, mesh.shape["dom"], mesh.shape["work"]),
        mesh=mesh,
        in_specs=(
            P(("dom", "work"), None),
            P(("dom", "work")),
            P(),
            P(("dom", "work")),
            P(("dom", "work")),
            P(("dom", "work")),
            P(),
            P(),
        ),
        out_specs=(P(("dom", "work"), None), P(("dom", "work"))),
        check_vma=False,
    )
```

```python
import functools
import math

import jax
import jax.numpy as jnp
from jax import lax
from jax.experimental import pallas as pl
from jax.experimental.pallas import tpu as pltpu
from jax.sharding import PartitionSpec as P

NEG = 1024
learn_rate = 0.1
MESH = pl.DeviceIdType.MESH
F32 = jnp.float32
BF16 = jnp.bfloat16
CODE = jnp.int16


def dot_nn(a, b):
    return lax.dot_general(a, b, (((1,), (0,)), ((), ())), preferred_element_type=F32)


def dot_nt(a, b):
    return lax.dot_general(a, b, (((1,), (1,)), ((), ())), preferred_element_type=F32)


def split(value):
    high = value.astype(BF16)
    low = (value - high.astype(F32)).astype(BF16)
    return high, low


def untranspose_pad(value):
    m, n = value.shape
    pad = -m % 128
    if pad:
        value = jnp.concatenate([value, jnp.zeros((pad, n), value.dtype)], axis=0)
    return jnp.transpose(value)[:, :m]


def encode(value):
    largest = jnp.max(jnp.abs(value), axis=0, keepdims=True)
    exponent = jnp.ceil(jnp.log2(jnp.maximum(largest, 1e-30)) + 0.03)
    exponent = jnp.broadcast_to(exponent, (16, value.shape[1]))
    scale = jnp.exp2(15.0 - exponent)[:1]
    code = jnp.floor(value * scale + 0.5).astype(jnp.int32)
    return code.astype(CODE), exponent.astype(jnp.int32).astype(CODE)


def store_code(ref, slot, value):
    rows = value.shape[0]
    code, exponent = encode(value)
    ref[slot, :rows, :] = code
    ref[slot, rows:, :] = exponent


def load_code(ref, slot):
    whole = ref[slot].astype(jnp.int32).astype(F32)
    rows = whole.shape[0] - 16
    scale = jnp.exp2(whole[rows:] - 15.0)[:1]
    return whole[:rows] * scale


class Exchange:
    def __init__(self, ref, device, a, b, a_size, b_size, sems):
        self.ref, self.device = ref, device
        self.a, self.b, self.a_size, self.b_size = a, b, a_size, b_size
        self.a_send, self.a_recv, self.b_send, self.b_recv = sems

    def slot(self, ka, kb):
        a = lax.rem(self.a + self.a_size - ka, self.a_size)
        b = lax.rem(self.b + self.b_size - kb, self.b_size)
        return a * self.b_size + b

    def peer(self, ka, kb):
        a = lax.rem(self.a + ka, self.a_size)
        b = lax.rem(self.b + kb, self.b_size)
        return self.device(a * self.b_size + b)

    def copy(self, slot, peer, send, recv):
        return pltpu.make_async_remote_copy(
            src_ref=self.ref.at[slot],
            dst_ref=self.ref.at[slot],
            send_sem=send,
            recv_sem=recv,
            device_id=peer,
            device_id_type=MESH,
        )

    def first(self, k, arriving=False):
        slot = self.slot(k, 0) if arriving else self.slot(0, 0)
        return self.copy(slot, self.peer(k, 0), self.a_send.at[k], self.a_recv.at[k])

    def second(self, ka, kb, arriving=False):
        slot = self.slot(ka, kb) if arriving else self.slot(ka, 0)
        at = ka * self.b_size + kb
        return self.copy(slot, self.peer(0, kb), self.b_send.at[at], self.b_recv.at[at])

    def start(self):
        for k in range(1, self.a_size):
            self.first(k).start()
        for kb in range(1, self.b_size):
            self.second(0, kb).start()

    def forward(self, k):
        self.first(k, True).wait_recv()
        for kb in range(1, self.b_size):
            self.second(k, kb).start()

    def collect(self):
        for ka in range(self.a_size):
            for kb in range(1, self.b_size):
                self.second(ka, kb, True).wait_recv()

    def finish(self):
        for k in range(1, self.a_size):
            self.first(k).wait_send()
        for ka in range(self.a_size):
            for kb in range(1, self.b_size):
                self.second(ka, kb).wait_send()


def kernel(
    dom_shape,
    work_shape,
    entity_ref,
    state_ref,
    relation_hbm,
    heads_ref,
    relations_ref,
    tails_ref,
    plan_ref,
    start_ref,
    entity_out,
    state_out,
    relation_vmem,
    parts,
    target_part,
    partial,
    own_partial,
    across,
    along_out,
    along_in,
    returned,
    rel_t,
    pulled,
    query_t,
    query_e,
    tail_hi,
    tail_lo,
    relation_sem,
    *sems,
):
    features, rows = entity_ref.shape
    half = features // 2
    edges = heads_ref.shape[1]
    relations = relation_hbm.shape[1]
    chips, cores = dom_shape
    z_size, x_size = work_shape
    part_rows = rows * z_size * x_size
    dom = lax.axis_index("dom")
    me = lax.axis_index("work")
    y, core = dom // cores, lax.rem(dom, cores)
    z, x = me // x_size, lax.rem(me, x_size)

    relation_copy = pltpu.make_async_copy(relation_hbm, relation_vmem, relation_sem)
    relation_copy.start()

    def dom_device(index):
        return (index, me)

    def work_device(index):
        return (dom, index)

    part_exchange = Exchange(parts, dom_device, y, core, chips, cores, sems[0:4])
    target_exchange = Exchange(target_part, work_device, z, x, z_size, x_size, sems[4:8])
    return_exchange = Exchange(returned, dom_device, y, core, chips, cores, sems[8:12])
    across_send, across_recv, along_send, along_recv = sems[12:16]

    barrier = pltpu.get_barrier_semaphore()
    for exchange in (part_exchange, target_exchange):
        for k in range(1, exchange.a_size):
            pl.semaphore_signal(
                barrier, inc=1, device_id=exchange.peer(k, 0), device_id_type=MESH
            )
        for k in range(1, exchange.b_size):
            pl.semaphore_signal(
                barrier, inc=1, device_id=exchange.peer(0, k), device_id_type=MESH
            )

    table_t = entity_ref[...].astype(BF16)
    parts[dom] = table_t
    pl.semaphore_wait(barrier, chips + cores + z_size + x_size - 4)
    part_exchange.start()

    head_local = heads_ref[...] - me * rows
    head_hot = (
        lax.broadcasted_iota(jnp.int32, (rows, edges), 0) == head_local
    ).astype(F32).astype(BF16)
    head_t = dot_nn(table_t, head_hot)

    for k in range(1, chips):
        part_exchange.forward(k)
    part_exchange.collect()
    target_part[me] = parts[plan_ref[dom]]
    target_exchange.start()

    relation_copy.wait()
    rel_t[...] = jnp.zeros_like(rel_t)
    step_rows = 256

    def relation_step(step, carry):
        base = pl.multiple_of(step * step_rows, step_rows)
        row = lax.broadcasted_iota(jnp.int32, (step_rows, edges), 0) + base
        hot = (row == relations_ref[...]).astype(F32).astype(BF16)
        rel_t[...] += dot_nn(relation_vmem[:, pl.ds(base, step_rows)], hot)
        return carry

    steps = relations // step_rows
    for k in range(1, z_size + 1):
        lax.fori_loop((k - 1) * steps // z_size, k * steps // z_size, relation_step, 0)
        if k < z_size:
            target_exchange.forward(k)

    rel_x, rel_y = rel_t[:half], rel_t[half:]
    head_x, head_y = head_t[:half], head_t[half:]
    query = jnp.concatenate(
        [head_x * rel_x - head_y * rel_y, head_x * rel_y + head_y * rel_x], axis=0
    )
    query_bf = query.astype(BF16)
    query_t[...] = query_bf
    query_float = query_bf.astype(F32)
    query_e[...] = untranspose_pad(query_float).astype(BF16)

    target_exchange.collect()

    width = x_size * rows

    def tail_hot(block):
        row = lax.broadcasted_iota(jnp.int32, (width, edges), 0) + block * width
        return (row == tails_ref[...]).astype(F32).astype(BF16)

    def block_of(block):
        return jnp.concatenate([target_part[block * x_size + j] for j in range(x_size)], axis=1)

    pulled[...] = jnp.zeros_like(pulled)

    def tail_step(block, carry):
        pulled[...] += dot_nn(block_of(block), tail_hot(block))
        return carry

    lax.fori_loop(0, z_size, tail_step, 0)
    tail_t = pulled[...]
    positive = jnp.sum(query_float * tail_t, axis=0, keepdims=True)
    positive_weight = jax.nn.sigmoid(positive) - 1.0
    pulled[...] = positive_weight * tail_t
    high, low = split(positive_weight * query_float)
    tail_hi[...] = high
    tail_lo[...] = low
    factor = 1.0 / math.sqrt(NEG)
    first_negative = start_ref[dom]

    def across_copy(block, j, arriving=False):
        k = lax.rem(j - x + x_size, x_size)
        landing = (lax.rem(x_size - k, x_size) if arriving else k) * z_size + block
        return pltpu.make_async_remote_copy(
            src_ref=partial.at[block * x_size + j],
            dst_ref=across.at[landing],
            send_sem=across_send.at[block * x_size + j],
            recv_sem=across_recv.at[landing],
            device_id=(dom, z * x_size + j),
            device_id_type=MESH,
        )

    def along_copy(k):
        return pltpu.make_async_remote_copy(
            src_ref=along_out.at[k],
            dst_ref=along_in.at[k],
            send_sem=along_send.at[k],
            recv_sem=along_recv.at[k],
            device_id=(dom, lax.rem(z + k, z_size) * x_size + x),
            device_id_type=MESH,
        )

    def score_step(step, carry):
        block = lax.rem(z + step + 1, z_size)
        part = block_of(block)
        scores = dot_nn(query_e[...], part)
        weights = jax.nn.sigmoid(scores) * factor
        if part_rows > NEG:
            row = lax.broadcasted_iota(jnp.int32, (1, width), 1) + block * width
            offset = row - first_negative
            offset = jnp.where(offset < 0, offset + part_rows, offset)
            weights = jnp.where(offset < NEG, weights, 0.0)
        weights = weights.astype(BF16)
        hot = tail_hot(block)
        grad = (
            dot_nn(query_t[...], weights) + dot_nt(tail_hi[...], hot) + dot_nt(tail_lo[...], hot)
        )
        for j in range(x_size):
            piece = grad[:, j * rows : (j + 1) * rows]

            @pl.when(x == j)
            def _():
                own_partial[block] = piece

            @pl.when(x != j)
            def _():
                store_code(partial, block * x_size + j, piece)
                across_copy(block, j).start()

        pulled[...] += dot_nt(part, weights)
        return carry

    lax.fori_loop(0, z_size, score_step, 0)

    def own_gradient():
        grad_x, grad_y = pulled[:half], pulled[half:]
        rel_x, rel_y = rel_t[:half], rel_t[half:]
        head_grad = jnp.concatenate(
            [grad_x * rel_x + grad_y * rel_y, grad_y * rel_x - grad_x * rel_y], axis=0
        )
        high, low = split(head_grad)
        return dot_nt(high, head_hot) + dot_nt(low, head_hot)

    own_grad = None
    for step in range(1, z_size + 1):
        block = lax.rem(z + step, z_size)
        total = own_partial[block]
        for k in range(1, x_size):
            across_copy(block, lax.rem(x + x_size - k, x_size), True).wait_recv()
            total = total + load_code(across, k * z_size + block)
        if step < z_size:
            store_code(along_out, step, total)
            along_copy(step).start()
        if step == 1:
            own_grad = own_gradient()
    for k in range(1, z_size):
        along_copy(k).wait_recv()
        total = total + load_code(along_in, k)
    store_code(returned, dom, total)
    return_exchange.start()
    giver = jnp.int32(0)
    for p in range(1, chips * cores):
        giver = jnp.where(plan_ref[p] == dom, jnp.int32(p), giver)
    for k in range(1, chips):
        return_exchange.forward(k)
    return_exchange.collect()
    gradient = own_grad + load_code(returned, giver)
    state_new = state_ref[...] + jnp.sum(gradient * gradient, axis=0, keepdims=True) / features
    state_out[...] = state_new
    entity_out[...] = entity_ref[...] - learn_rate * gradient / jnp.sqrt(state_new)

    part_exchange.finish()
    target_exchange.finish()
    return_exchange.finish()
    for k in range(1, z_size):
        along_copy(k).wait_send()
    for block in range(z_size):
        for k in range(1, x_size):
            across_copy(block, lax.rem(x + k, x_size)).wait_send()


def body(
    dom_shape,
    work_shape,
    entity,
    row_state,
    relation_table,
    edge_heads,
    edge_relations,
    edge_tails,
    plan,
    negative_start,
):
    rows, features = entity.shape
    edges = edge_heads.shape[0]
    chips, cores = dom_shape
    z_size, x_size = work_shape
    domains, workers = chips * cores, z_size * x_size
    vmem = pl.BlockSpec(memory_space=pltpu.VMEM)
    smem = pl.BlockSpec(memory_space=pltpu.SMEM)
    coded = (features + 16, rows)
    counts = (
        [chips, chips, domains, domains]
        + [z_size, z_size, workers, workers]
        + [chips, chips, domains, domains]
        + [workers, workers, z_size, z_size]
    )
    entity_new, state_new = pl.pallas_call(
        functools.partial(kernel, dom_shape, work_shape),
        out_shape=(
            jax.ShapeDtypeStruct((features, rows), F32),
            jax.ShapeDtypeStruct((1, rows), F32),
        ),
        in_specs=[vmem, vmem, pl.BlockSpec(memory_space=pl.ANY), vmem, vmem, vmem, smem, smem],
        out_specs=(vmem, vmem),
        scratch_shapes=[
            pltpu.VMEM(relation_table.shape[::-1], BF16),
            pltpu.VMEM((domains, features, rows), BF16),
            pltpu.VMEM((workers, features, rows), BF16),
            pltpu.VMEM((workers,) + coded, CODE),
            pltpu.VMEM((z_size, features, rows), F32),
            pltpu.VMEM((workers,) + coded, CODE),
            pltpu.VMEM((z_size,) + coded, CODE),
            pltpu.VMEM((z_size,) + coded, CODE),
            pltpu.VMEM((domains,) + coded, CODE),
            pltpu.VMEM((features, edges), F32),
            pltpu.VMEM((features, edges), F32),
            pltpu.VMEM((features, edges), BF16),
            pltpu.VMEM((edges, features), BF16),
            pltpu.VMEM((features, edges), BF16),
            pltpu.VMEM((features, edges), BF16),
            pltpu.SemaphoreType.DMA,
        ]
        + [pltpu.SemaphoreType.DMA((count,)) for count in counts],
        compiler_params=pltpu.CompilerParams(
            collective_id=0, has_side_effects=True, vmem_limit_bytes=50 << 20
        ),
    )(
        entity.T,
        row_state.reshape(1, rows),
        relation_table.T,
        edge_heads.reshape(1, edges),
        edge_relations.reshape(1, edges),
        edge_tails.reshape(1, edges),
        plan,
        negative_start,
    )
    return entity_new.T, state_new.reshape(rows)


def axis_shapes(mesh):
    domains, workers = mesh.shape["dom"], mesh.shape["work"]
    cores = 2 if domains % 2 == 0 else 1
    x_size = max(math.isqrt(workers // 2), 1)
    while workers % x_size:
        x_size -= 1
    return (domains // cores, cores), (workers // x_size, x_size)


def solution(mesh):
    return jax.shard_map(
        functools.partial(body, *axis_shapes(mesh)),
        mesh=mesh,
        in_specs=(
            P(("dom", "work"), None),
            P(("dom", "work")),
            P(),
            P(("dom", "work")),
            P(("dom", "work")),
            P(("dom", "work")),
            P(),
            P(),
        ),
        out_specs=(P(("dom", "work"), None), P(("dom", "work"))),
        check_vma=False,
    )
```

```python
import functools
import math

import jax
import jax.numpy as jnp
from jax import lax
from jax.experimental import pallas as pl
from jax.experimental.pallas import tpu as pltpu
from jax.sharding import PartitionSpec as P

NEG = 1024
learn_rate = 0.1
MESH = pl.DeviceIdType.MESH
F32 = jnp.float32
BF16 = jnp.bfloat16
CODE = jnp.int16


def dot_nn(a, b):
    return lax.dot_general(a, b, (((1,), (0,)), ((), ())), preferred_element_type=F32)


def dot_nt(a, b):
    return lax.dot_general(a, b, (((1,), (1,)), ((), ())), preferred_element_type=F32)


def split(value):
    high = value.astype(BF16)
    low = (value - high.astype(F32)).astype(BF16)
    return high, low


def untranspose_pad(value):
    m, n = value.shape
    pad = -m % 128
    if pad:
        value = jnp.concatenate([value, jnp.zeros((pad, n), value.dtype)], axis=0)
    return jnp.transpose(value)[:, :m]


def encode(value):
    largest = jnp.max(jnp.abs(value), axis=0, keepdims=True)
    exponent = jnp.ceil(jnp.log2(jnp.maximum(largest, 1e-30)) + 0.03)
    exponent = jnp.broadcast_to(exponent, (16, value.shape[1]))
    scale = jnp.exp2(15.0 - exponent)[:1]
    code = jnp.floor(value * scale + 0.5).astype(jnp.int32)
    return code.astype(CODE), exponent.astype(jnp.int32).astype(CODE)


def store_code(ref, slot, value):
    rows = value.shape[0]
    code, exponent = encode(value)
    ref[slot, :rows, :] = code
    ref[slot, rows:, :] = exponent


def load_code(ref, slot):
    whole = ref[slot].astype(jnp.int32).astype(F32)
    rows = whole.shape[0] - 16
    scale = jnp.exp2(whole[rows:] - 15.0)[:1]
    return whole[:rows] * scale


class Exchange:
    def __init__(self, ref, device, a, b, a_size, b_size, sems):
        self.ref, self.device = ref, device
        self.a, self.b, self.a_size, self.b_size = a, b, a_size, b_size
        self.a_send, self.a_recv, self.b_send, self.b_recv = sems

    def slot(self, ka, kb):
        a = lax.rem(self.a + self.a_size - ka, self.a_size)
        b = lax.rem(self.b + self.b_size - kb, self.b_size)
        return a * self.b_size + b

    def peer(self, ka, kb):
        a = lax.rem(self.a + ka, self.a_size)
        b = lax.rem(self.b + kb, self.b_size)
        return self.device(a * self.b_size + b)

    def copy(self, slot, peer, send, recv):
        return pltpu.make_async_remote_copy(
            src_ref=self.ref.at[slot],
            dst_ref=self.ref.at[slot],
            send_sem=send,
            recv_sem=recv,
            device_id=peer,
            device_id_type=MESH,
        )

    def first(self, k, arriving=False):
        slot = self.slot(k, 0) if arriving else self.slot(0, 0)
        return self.copy(slot, self.peer(k, 0), self.a_send.at[k], self.a_recv.at[k])

    def second(self, ka, kb, arriving=False):
        slot = self.slot(ka, kb) if arriving else self.slot(ka, 0)
        at = ka * self.b_size + kb
        return self.copy(slot, self.peer(0, kb), self.b_send.at[at], self.b_recv.at[at])

    def start(self):
        for k in range(1, self.a_size):
            self.first(k).start()
        for kb in range(1, self.b_size):
            self.second(0, kb).start()

    def forward(self, k):
        self.first(k, True).wait_recv()
        for kb in range(1, self.b_size):
            self.second(k, kb).start()

    def collect(self):
        for ka in range(self.a_size):
            for kb in range(1, self.b_size):
                self.second(ka, kb, True).wait_recv()

    def finish(self):
        for k in range(1, self.a_size):
            self.first(k).wait_send()
        for ka in range(self.a_size):
            for kb in range(1, self.b_size):
                self.second(ka, kb).wait_send()


def kernel(
    dom_shape,
    work_shape,
    entity_hbm,
    state_hbm,
    relation_hbm,
    heads_hbm,
    relations_hbm,
    tails_hbm,
    plan_hbm,
    start_hbm,
    entity_out,
    state_out,
    entity_ref,
    state_ref,
    relation_vmem,
    heads_ref,
    relations_ref,
    tails_ref,
    plan_ref,
    start_ref,
    parts,
    target_part,
    partial,
    own_partial,
    negative,
    across,
    along_out,
    along_in,
    returned,
    rel_t,
    tail_rows,
    pulled,
    query_t,
    query_e,
    tail_hi,
    tail_lo,
    load_sem,
    *sems,
):
    features, rows = entity_hbm.shape
    half = features // 2
    edges = heads_hbm.shape[1]
    relations = relation_hbm.shape[1]
    chips, cores = dom_shape
    z_size, x_size = work_shape
    part_rows = rows * z_size * x_size
    dom = lax.axis_index("dom")
    me = lax.axis_index("work")
    y, core = dom // cores, lax.rem(dom, cores)
    z, x = me // x_size, lax.rem(me, x_size)

    pairs = (
        (entity_hbm, entity_ref),
        (heads_hbm, heads_ref),
        (relations_hbm, relations_ref),
        (tails_hbm, tails_ref),
        (plan_hbm, plan_ref),
        (start_hbm, start_ref),
        (state_hbm, state_ref),
        (relation_hbm, relation_vmem),
    )
    loads = [
        pltpu.make_async_copy(source, to, load_sem.at[i]) for i, (source, to) in enumerate(pairs)
    ]
    for load in loads:
        load.start()

    def dom_device(index):
        return (index, me)

    def work_device(index):
        return (dom, index)

    part_exchange = Exchange(parts, dom_device, y, core, chips, cores, sems[0:4])
    target_exchange = Exchange(target_part, work_device, z, x, z_size, x_size, sems[4:8])
    return_exchange = Exchange(returned, dom_device, y, core, chips, cores, sems[8:12])
    across_send, across_recv, along_send, along_recv = sems[12:16]

    barrier = pltpu.get_barrier_semaphore()
    for exchange in (part_exchange, target_exchange):
        for k in range(1, exchange.a_size):
            pl.semaphore_signal(
                barrier, inc=1, device_id=exchange.peer(k, 0), device_id_type=MESH
            )
        for k in range(1, exchange.b_size):
            pl.semaphore_signal(
                barrier, inc=1, device_id=exchange.peer(0, k), device_id_type=MESH
            )

    loads[0].wait()
    table_t = entity_ref[...].astype(BF16)
    parts[dom] = table_t
    pl.semaphore_wait(barrier, chips + cores + z_size + x_size - 4)
    part_exchange.start()

    for load in loads[1:]:
        load.wait()
    head_local = heads_ref[...] - me * rows
    head_hot = (
        lax.broadcasted_iota(jnp.int32, (rows, edges), 0) == head_local
    ).astype(F32).astype(BF16)
    head_t = dot_nn(table_t, head_hot)

    rel_t[...] = jnp.zeros_like(rel_t)
    step_rows = 256

    def relation_step(step, carry):
        base = pl.multiple_of(step * step_rows, step_rows)
        row = lax.broadcasted_iota(jnp.int32, (step_rows, edges), 0) + base
        hot = (row == relations_ref[...]).astype(F32).astype(BF16)
        rel_t[...] += dot_nn(relation_vmem[:, pl.ds(base, step_rows)], hot)
        return carry

    steps = relations // step_rows
    for k in range(1, chips + 1):
        lax.fori_loop((k - 1) * steps // chips, k * steps // chips, relation_step, 0)
        if k < chips:
            part_exchange.forward(k)
    part_exchange.collect()
    target_part[me] = parts[plan_ref[dom]]
    target_exchange.start()

    rel_x, rel_y = rel_t[:half], rel_t[half:]
    head_x, head_y = head_t[:half], head_t[half:]
    query = jnp.concatenate(
        [head_x * rel_x - head_y * rel_y, head_x * rel_y + head_y * rel_x], axis=0
    )
    query_bf = query.astype(BF16)
    query_t[...] = query_bf
    query_float = query_bf.astype(F32)
    query_e[...] = untranspose_pad(query_float).astype(BF16)

    width = x_size * rows
    factor = 1.0 / math.sqrt(NEG)
    first_negative = start_ref[dom]

    def tail_hot(block):
        row = lax.broadcasted_iota(jnp.int32, (width, edges), 0) + block * width
        return (row == tails_ref[...]).astype(F32).astype(BF16)

    tail_rows[...] = jnp.zeros_like(tail_rows)
    pulled[...] = jnp.zeros_like(pulled)

    def score_step(k, carry):
        @pl.when(k < z_size - 1)
        def _():
            target_exchange.forward(k + 1)

        for kb in range(1, x_size):
            target_exchange.second(k, kb, True).wait_recv()
        block = lax.rem(z + z_size - k, z_size)
        part = jnp.concatenate(
            [target_part[block * x_size + j] for j in range(x_size)], axis=1
        )
        tail_rows[...] += dot_nn(part, tail_hot(block))
        scores = dot_nn(query_e[...], part)
        weights = jax.nn.sigmoid(scores) * factor
        if part_rows > NEG:
            row = lax.broadcasted_iota(jnp.int32, (1, width), 1) + block * width
            offset = row - first_negative
            offset = jnp.where(offset < 0, offset + part_rows, offset)
            weights = jnp.where(offset < NEG, weights, 0.0)
        weights = weights.astype(BF16)
        pulled[...] += dot_nt(part, weights)
        negative[block] = dot_nn(query_t[...], weights)
        return carry

    lax.fori_loop(0, z_size, score_step, 0)
    tail_t = tail_rows[...]
    positive = jnp.sum(query_float * tail_t, axis=0, keepdims=True)
    positive_weight = jax.nn.sigmoid(positive) - 1.0
    high, low = split(positive_weight * query_float)
    tail_hi[...] = high
    tail_lo[...] = low

    def across_copy(block, j, arriving=False):
        k = lax.rem(j - x + x_size, x_size)
        landing = (lax.rem(x_size - k, x_size) if arriving else k) * z_size + block
        return pltpu.make_async_remote_copy(
            src_ref=partial.at[block * x_size + j],
            dst_ref=across.at[landing],
            send_sem=across_send.at[block * x_size + j],
            recv_sem=across_recv.at[landing],
            device_id=(dom, z * x_size + j),
            device_id_type=MESH,
        )

    def along_copy(k):
        return pltpu.make_async_remote_copy(
            src_ref=along_out.at[k],
            dst_ref=along_in.at[k],
            send_sem=along_send.at[k],
            recv_sem=along_recv.at[k],
            device_id=(dom, lax.rem(z + k, z_size) * x_size + x),
            device_id_type=MESH,
        )

    def send_step(step, carry):
        block = lax.rem(z + step + 1, z_size)
        hot = tail_hot(block)
        grad = negative[block] + dot_nt(tail_hi[...], hot) + dot_nt(tail_lo[...], hot)
        for j in range(x_size):
            piece = grad[:, j * rows : (j + 1) * rows]

            @pl.when(x == j)
            def _():
                own_partial[block] = piece

            @pl.when(x != j)
            def _():
                store_code(partial, block * x_size + j, piece)
                across_copy(block, j).start()

        return carry

    lax.fori_loop(0, z_size, send_step, 0)

    def own_gradient():
        grad_t = positive_weight * tail_rows[...] + pulled[...]
        grad_x, grad_y = grad_t[:half], grad_t[half:]
        rel_x, rel_y = rel_t[:half], rel_t[half:]
        head_grad = jnp.concatenate(
            [grad_x * rel_x + grad_y * rel_y, grad_y * rel_x - grad_x * rel_y], axis=0
        )
        high, low = split(head_grad)
        return dot_nt(high, head_hot) + dot_nt(low, head_hot)

    own_grad = None
    for step in range(1, z_size + 1):
        block = lax.rem(z + step, z_size)
        total = own_partial[block]
        for k in range(1, x_size):
            across_copy(block, lax.rem(x + x_size - k, x_size), True).wait_recv()
            total = total + load_code(across, k * z_size + block)
        if step < z_size:
            store_code(along_out, step, total)
            along_copy(step).start()
        if step == 1:
            own_grad = own_gradient()
    for k in range(1, z_size):
        along_copy(k).wait_recv()
        total = total + load_code(along_in, k)
    store_code(returned, dom, total)
    return_exchange.start()
    giver = jnp.int32(0)
    for p in range(1, chips * cores):
        giver = jnp.where(plan_ref[p] == dom, jnp.int32(p), giver)
    for k in range(1, chips):
        return_exchange.forward(k)
    return_exchange.collect()
    gradient = own_grad + load_code(returned, giver)
    state_new = state_ref[...] + jnp.sum(gradient * gradient, axis=0, keepdims=True) / features
    state_out[...] = state_new
    entity_out[...] = entity_ref[...] - learn_rate * gradient / jnp.sqrt(state_new)

    part_exchange.finish()
    target_exchange.finish()
    return_exchange.finish()
    for k in range(1, z_size):
        along_copy(k).wait_send()
    for block in range(z_size):
        for k in range(1, x_size):
            across_copy(block, lax.rem(x + k, x_size)).wait_send()


def body(
    dom_shape,
    work_shape,
    entity,
    row_state,
    relation_table,
    edge_heads,
    edge_relations,
    edge_tails,
    plan,
    negative_start,
):
    rows, features = entity.shape
    edges = edge_heads.shape[0]
    chips, cores = dom_shape
    z_size, x_size = work_shape
    domains, workers = chips * cores, z_size * x_size
    vmem = pl.BlockSpec(memory_space=pltpu.VMEM)
    coded = (features + 16, rows)
    counts = (
        [chips, chips, domains, domains]
        + [z_size, z_size, workers, workers]
        + [chips, chips, domains, domains]
        + [workers, workers, z_size, z_size]
    )
    entity_new, state_new = pl.pallas_call(
        functools.partial(kernel, dom_shape, work_shape),
        out_shape=(
            jax.ShapeDtypeStruct((features, rows), F32),
            jax.ShapeDtypeStruct((1, rows), F32),
        ),
        in_specs=[pl.BlockSpec(memory_space=pltpu.HBM)] * 8,
        out_specs=(vmem, vmem),
        scratch_shapes=[
            pltpu.VMEM((features, rows), F32),
            pltpu.VMEM((1, rows), F32),
            pltpu.VMEM(relation_table.shape[::-1], BF16),
            pltpu.VMEM((1, edges), jnp.int32),
            pltpu.VMEM((1, edges), jnp.int32),
            pltpu.VMEM((1, edges), jnp.int32),
            pltpu.SMEM(plan.shape, jnp.int32),
            pltpu.SMEM(negative_start.shape, jnp.int32),
            pltpu.VMEM((domains, features, rows), BF16),
            pltpu.VMEM((workers, features, rows), BF16),
            pltpu.VMEM((workers,) + coded, CODE),
            pltpu.VMEM((z_size, features, rows), F32),
            pltpu.VMEM((z_size, features, x_size * rows), F32),
            pltpu.VMEM((workers,) + coded, CODE),
            pltpu.VMEM((z_size,) + coded, CODE),
            pltpu.VMEM((z_size,) + coded, CODE),
            pltpu.VMEM((domains,) + coded, CODE),
            pltpu.VMEM((features, edges), F32),
            pltpu.VMEM((features, edges), F32),
            pltpu.VMEM((features, edges), F32),
            pltpu.VMEM((features, edges), BF16),
            pltpu.VMEM((edges, features), BF16),
            pltpu.VMEM((features, edges), BF16),
            pltpu.VMEM((features, edges), BF16),
            pltpu.SemaphoreType.DMA((8,)),
        ]
        + [pltpu.SemaphoreType.DMA((count,)) for count in counts],
        compiler_params=pltpu.CompilerParams(
            collective_id=0, has_side_effects=True, vmem_limit_bytes=56 << 20
        ),
    )(
        entity.T,
        row_state.reshape(1, rows),
        relation_table.T,
        edge_heads.reshape(1, edges),
        edge_relations.reshape(1, edges),
        edge_tails.reshape(1, edges),
        plan,
        negative_start,
    )
    return entity_new.T, state_new.reshape(rows)


def axis_shapes(mesh):
    domains, workers = mesh.shape["dom"], mesh.shape["work"]
    cores = 2 if domains % 2 == 0 else 1
    x_size = max(math.isqrt(workers // 2), 1)
    while workers % x_size:
        x_size -= 1
    return (domains // cores, cores), (workers // x_size, x_size)


def solution(mesh):
    return jax.shard_map(
        functools.partial(body, *axis_shapes(mesh)),
        mesh=mesh,
        in_specs=(
            P(("dom", "work"), None),
            P(("dom", "work")),
            P(),
            P(("dom", "work")),
            P(("dom", "work")),
            P(("dom", "work")),
            P(),
            P(),
        ),
        out_specs=(P(("dom", "work"), None), P(("dom", "work"))),
        check_vma=False,
    )
```

```python
import functools
import math

import jax
import jax.numpy as jnp
from jax import lax
from jax.experimental import pallas as pl
from jax.experimental.pallas import tpu as pltpu
from jax.sharding import PartitionSpec as P

NEG = 1024
learn_rate = 0.1
MESH = pl.DeviceIdType.MESH
F32 = jnp.float32
BF16 = jnp.bfloat16
CODE = jnp.int16


def dot_nn(a, b):
    return lax.dot_general(a, b, (((1,), (0,)), ((), ())), preferred_element_type=F32)


def dot_nt(a, b):
    return lax.dot_general(a, b, (((1,), (1,)), ((), ())), preferred_element_type=F32)


def split(value):
    high = value.astype(BF16)
    low = (value - high.astype(F32)).astype(BF16)
    return high, low


def untranspose_pad(value):
    m, n = value.shape
    pad = -m % 128
    if pad:
        value = jnp.concatenate([value, jnp.zeros((pad, n), value.dtype)], axis=0)
    return jnp.transpose(value)[:, :m]


def encode(value):
    largest = jnp.max(jnp.abs(value), axis=0, keepdims=True)
    exponent = jnp.ceil(jnp.log2(jnp.maximum(largest, 1e-30)) + 0.03)
    exponent = jnp.broadcast_to(exponent, (16, value.shape[1]))
    scale = jnp.exp2(15.0 - exponent)[:1]
    code = jnp.floor(value * scale + 0.5).astype(jnp.int32)
    return code.astype(CODE), exponent.astype(jnp.int32).astype(CODE)


def store_code(ref, slot, value):
    rows = value.shape[0]
    code, exponent = encode(value)
    ref[slot, :rows, :] = code
    ref[slot, rows:, :] = exponent


def load_code(ref, slot):
    whole = ref[slot].astype(jnp.int32).astype(F32)
    rows = whole.shape[0] - 16
    scale = jnp.exp2(whole[rows:] - 15.0)[:1]
    return whole[:rows] * scale


class Exchange:
    def __init__(self, ref, device, a, b, a_size, b_size, sems):
        self.ref, self.device = ref, device
        self.a, self.b, self.a_size, self.b_size = a, b, a_size, b_size
        self.a_send, self.a_recv, self.b_send, self.b_recv = sems

    def slot(self, ka, kb):
        a = lax.rem(self.a + self.a_size - ka, self.a_size)
        b = lax.rem(self.b + self.b_size - kb, self.b_size)
        return a * self.b_size + b

    def peer(self, ka, kb):
        a = lax.rem(self.a + ka, self.a_size)
        b = lax.rem(self.b + kb, self.b_size)
        return self.device(a * self.b_size + b)

    def copy(self, slot, peer, send, recv):
        return pltpu.make_async_remote_copy(
            src_ref=self.ref.at[slot],
            dst_ref=self.ref.at[slot],
            send_sem=send,
            recv_sem=recv,
            device_id=peer,
            device_id_type=MESH,
        )

    def first(self, k, arriving=False):
        slot = self.slot(k, 0) if arriving else self.slot(0, 0)
        return self.copy(slot, self.peer(k, 0), self.a_send.at[k], self.a_recv.at[k])

    def second(self, ka, kb, arriving=False):
        slot = self.slot(ka, kb) if arriving else self.slot(ka, 0)
        at = ka * self.b_size + kb
        return self.copy(slot, self.peer(0, kb), self.b_send.at[at], self.b_recv.at[at])

    def start(self):
        for k in range(1, self.a_size):
            self.first(k).start()
        for kb in range(1, self.b_size):
            self.second(0, kb).start()

    def forward(self, k):
        self.first(k, True).wait_recv()
        for kb in range(1, self.b_size):
            self.second(k, kb).start()

    def collect(self):
        for ka in range(self.a_size):
            for kb in range(1, self.b_size):
                self.second(ka, kb, True).wait_recv()

    def finish(self):
        for k in range(1, self.a_size):
            self.first(k).wait_send()
        for ka in range(self.a_size):
            for kb in range(1, self.b_size):
                self.second(ka, kb).wait_send()


def kernel(
    dom_shape,
    work_shape,
    entity_hbm,
    state_hbm,
    relation_hbm,
    heads_hbm,
    relations_hbm,
    tails_hbm,
    plan_hbm,
    start_hbm,
    entity_out,
    state_out,
    entity_ref,
    state_ref,
    relation_vmem,
    heads_ref,
    relations_ref,
    tails_ref,
    plan_ref,
    start_ref,
    parts,
    target_part,
    partial,
    own_partial,
    negative,
    across,
    along_out,
    along_in,
    returned,
    rel_t,
    tail_rows,
    pulled,
    query_t,
    query_e,
    tail_hi,
    tail_lo,
    load_sem,
    *sems,
):
    features, rows = entity_hbm.shape
    half = features // 2
    edges = heads_hbm.shape[1]
    relations = relation_hbm.shape[1]
    chips, cores = dom_shape
    z_size, x_size = work_shape
    part_rows = rows * z_size * x_size
    dom = lax.axis_index("dom")
    me = lax.axis_index("work")
    y, core = dom // cores, lax.rem(dom, cores)
    z, x = me // x_size, lax.rem(me, x_size)

    pairs = (
        (entity_hbm, entity_ref),
        (heads_hbm, heads_ref),
        (relations_hbm, relations_ref),
        (tails_hbm, tails_ref),
        (plan_hbm, plan_ref),
        (start_hbm, start_ref),
        (state_hbm, state_ref),
        (relation_hbm, relation_vmem),
    )
    loads = [
        pltpu.make_async_copy(source, to, load_sem.at[i]) for i, (source, to) in enumerate(pairs)
    ]
    for load in loads:
        load.start()

    def dom_device(index):
        return (index, me)

    def work_device(index):
        return (dom, index)

    part_exchange = Exchange(parts, dom_device, y, core, chips, cores, sems[0:4])
    target_exchange = Exchange(target_part, work_device, z, x, z_size, x_size, sems[4:8])
    return_exchange = Exchange(returned, dom_device, y, core, chips, cores, sems[8:12])
    across_send, across_recv, along_send, along_recv = sems[12:16]

    barrier = pltpu.get_barrier_semaphore()
    for exchange in (part_exchange, target_exchange):
        for k in range(1, exchange.a_size):
            pl.semaphore_signal(
                barrier, inc=1, device_id=exchange.peer(k, 0), device_id_type=MESH
            )
        for k in range(1, exchange.b_size):
            pl.semaphore_signal(
                barrier, inc=1, device_id=exchange.peer(0, k), device_id_type=MESH
            )

    loads[0].wait()
    table_t = entity_ref[...].astype(BF16)
    parts[dom] = table_t
    pl.semaphore_wait(barrier, chips + cores + z_size + x_size - 4)
    part_exchange.start()

    for load in loads[1:]:
        load.wait()
    head_local = heads_ref[...] - me * rows
    head_hot = (
        lax.broadcasted_iota(jnp.int32, (rows, edges), 0) == head_local
    ).astype(F32).astype(BF16)
    head_t = dot_nn(table_t, head_hot)

    rel_t[...] = jnp.zeros_like(rel_t)
    step_rows = 512

    def relation_step(step, carry):
        base = pl.multiple_of(step * step_rows, step_rows)
        row = lax.broadcasted_iota(jnp.int32, (step_rows, edges), 0) + base
        hot = (row == relations_ref[...]).astype(F32).astype(BF16)
        rel_t[...] += dot_nn(relation_vmem[:, pl.ds(base, step_rows)], hot)
        return carry

    steps = relations // step_rows
    for k in range(1, chips + 1):
        lax.fori_loop((k - 1) * steps // chips, k * steps // chips, relation_step, 0)
        if k < chips:
            part_exchange.forward(k)
    part_exchange.collect()
    target_part[me] = parts[plan_ref[dom]]
    target_exchange.start()

    rel_x, rel_y = rel_t[:half], rel_t[half:]
    head_x, head_y = head_t[:half], head_t[half:]
    query = jnp.concatenate(
        [head_x * rel_x - head_y * rel_y, head_x * rel_y + head_y * rel_x], axis=0
    )
    query_bf = query.astype(BF16)
    query_t[...] = query_bf
    query_float = query_bf.astype(F32)
    query_e[...] = untranspose_pad(query_float).astype(BF16)

    width = x_size * rows
    factor = 1.0 / math.sqrt(NEG)
    first_negative = start_ref[dom]

    def tail_hot(block):
        row = lax.broadcasted_iota(jnp.int32, (width, edges), 0) + block * width
        return (row == tails_ref[...]).astype(F32).astype(BF16)

    tail_rows[...] = jnp.zeros_like(tail_rows)
    pulled[...] = jnp.zeros_like(pulled)

    def score_step(k, carry):
        @pl.when(k < z_size - 1)
        def _():
            target_exchange.forward(k + 1)

        for kb in range(1, x_size):
            target_exchange.second(k, kb, True).wait_recv()
        block = lax.rem(z + z_size - k, z_size)
        part = jnp.concatenate(
            [target_part[block * x_size + j] for j in range(x_size)], axis=1
        )
        tail_rows[...] += dot_nn(part, tail_hot(block))
        scores = dot_nn(query_e[...], part)
        weights = jax.nn.sigmoid(scores) * factor
        if part_rows > NEG:
            row = lax.broadcasted_iota(jnp.int32, (1, width), 1) + block * width
            offset = row - first_negative
            offset = jnp.where(offset < 0, offset + part_rows, offset)
            weights = jnp.where(offset < NEG, weights, 0.0)
        weights = weights.astype(BF16)
        pulled[...] += dot_nt(part, weights)
        negative[block] = dot_nn(query_t[...], weights)
        return carry

    lax.fori_loop(0, z_size, score_step, 0)
    tail_t = tail_rows[...]
    positive = jnp.sum(query_float * tail_t, axis=0, keepdims=True)
    positive_weight = jax.nn.sigmoid(positive) - 1.0
    high, low = split(positive_weight * query_float)
    tail_hi[...] = high
    tail_lo[...] = low

    def across_copy(block, j, arriving=False):
        k = lax.rem(j - x + x_size, x_size)
        landing = (lax.rem(x_size - k, x_size) if arriving else k) * z_size + block
        return pltpu.make_async_remote_copy(
            src_ref=partial.at[block * x_size + j],
            dst_ref=across.at[landing],
            send_sem=across_send.at[block * x_size + j],
            recv_sem=across_recv.at[landing],
            device_id=(dom, z * x_size + j),
            device_id_type=MESH,
        )

    def along_copy(k):
        return pltpu.make_async_remote_copy(
            src_ref=along_out.at[k],
            dst_ref=along_in.at[k],
            send_sem=along_send.at[k],
            recv_sem=along_recv.at[k],
            device_id=(dom, lax.rem(z + k, z_size) * x_size + x),
            device_id_type=MESH,
        )

    def send_step(step, carry):
        block = lax.rem(z + step + 1, z_size)
        hot = tail_hot(block)
        grad = negative[block] + dot_nt(tail_hi[...], hot) + dot_nt(tail_lo[...], hot)
        for j in range(x_size):
            piece = grad[:, j * rows : (j + 1) * rows]

            @pl.when(x == j)
            def _():
                own_partial[block] = piece

            @pl.when(x != j)
            def _():
                store_code(partial, block * x_size + j, piece)
                across_copy(block, j).start()

        return carry

    lax.fori_loop(0, z_size, send_step, 0)

    def own_gradient():
        grad_t = positive_weight * tail_rows[...] + pulled[...]
        grad_x, grad_y = grad_t[:half], grad_t[half:]
        rel_x, rel_y = rel_t[:half], rel_t[half:]
        head_grad = jnp.concatenate(
            [grad_x * rel_x + grad_y * rel_y, grad_y * rel_x - grad_x * rel_y], axis=0
        )
        high, low = split(head_grad)
        return dot_nt(high, head_hot) + dot_nt(low, head_hot)

    own_grad = None
    for step in range(1, z_size + 1):
        block = lax.rem(z + step, z_size)
        total = own_partial[block]
        for k in range(1, x_size):
            across_copy(block, lax.rem(x + x_size - k, x_size), True).wait_recv()
            total = total + load_code(across, k * z_size + block)
        if step < z_size:
            store_code(along_out, step, total)
            along_copy(step).start()
        if step == z_size - 1:
            own_grad = own_gradient()
    for k in range(1, z_size):
        along_copy(k).wait_recv()
        total = total + load_code(along_in, k)
    store_code(returned, dom, total)
    return_exchange.start()
    giver = jnp.int32(0)
    for p in range(1, chips * cores):
        giver = jnp.where(plan_ref[p] == dom, jnp.int32(p), giver)
    for k in range(1, chips):
        return_exchange.forward(k)
    return_exchange.collect()
    gradient = own_grad + load_code(returned, giver)
    state_new = state_ref[...] + jnp.sum(gradient * gradient, axis=0, keepdims=True) / features
    state_out[...] = state_new
    entity_out[...] = entity_ref[...] - learn_rate * gradient / jnp.sqrt(state_new)

    part_exchange.finish()
    target_exchange.finish()
    return_exchange.finish()
    for k in range(1, z_size):
        along_copy(k).wait_send()
    for block in range(z_size):
        for k in range(1, x_size):
            across_copy(block, lax.rem(x + k, x_size)).wait_send()


def body(
    dom_shape,
    work_shape,
    entity,
    row_state,
    relation_table,
    edge_heads,
    edge_relations,
    edge_tails,
    plan,
    negative_start,
):
    rows, features = entity.shape
    edges = edge_heads.shape[0]
    chips, cores = dom_shape
    z_size, x_size = work_shape
    domains, workers = chips * cores, z_size * x_size
    vmem = pl.BlockSpec(memory_space=pltpu.VMEM)
    coded = (features + 16, rows)
    counts = (
        [chips, chips, domains, domains]
        + [z_size, z_size, workers, workers]
        + [chips, chips, domains, domains]
        + [workers, workers, z_size, z_size]
    )
    entity_new, state_new = pl.pallas_call(
        functools.partial(kernel, dom_shape, work_shape),
        out_shape=(
            jax.ShapeDtypeStruct((features, rows), F32),
            jax.ShapeDtypeStruct((1, rows), F32),
        ),
        in_specs=[pl.BlockSpec(memory_space=pltpu.HBM)] * 8,
        out_specs=(vmem, vmem),
        scratch_shapes=[
            pltpu.VMEM((features, rows), F32),
            pltpu.VMEM((1, rows), F32),
            pltpu.VMEM(relation_table.shape[::-1], BF16),
            pltpu.VMEM((1, edges), jnp.int32),
            pltpu.VMEM((1, edges), jnp.int32),
            pltpu.VMEM((1, edges), jnp.int32),
            pltpu.SMEM(plan.shape, jnp.int32),
            pltpu.SMEM(negative_start.shape, jnp.int32),
            pltpu.VMEM((domains, features, rows), BF16),
            pltpu.VMEM((workers, features, rows), BF16),
            pltpu.VMEM((workers,) + coded, CODE),
            pltpu.VMEM((z_size, features, rows), F32),
            pltpu.VMEM((z_size, features, x_size * rows), F32),
            pltpu.VMEM((workers,) + coded, CODE),
            pltpu.VMEM((z_size,) + coded, CODE),
            pltpu.VMEM((z_size,) + coded, CODE),
            pltpu.VMEM((domains,) + coded, CODE),
            pltpu.VMEM((features, edges), F32),
            pltpu.VMEM((features, edges), F32),
            pltpu.VMEM((features, edges), F32),
            pltpu.VMEM((features, edges), BF16),
            pltpu.VMEM((edges, features), BF16),
            pltpu.VMEM((features, edges), BF16),
            pltpu.VMEM((features, edges), BF16),
            pltpu.SemaphoreType.DMA((8,)),
        ]
        + [pltpu.SemaphoreType.DMA((count,)) for count in counts],
        compiler_params=pltpu.CompilerParams(
            collective_id=0, has_side_effects=True, vmem_limit_bytes=56 << 20
        ),
    )(
        entity.T,
        row_state.reshape(1, rows),
        relation_table.T,
        edge_heads.reshape(1, edges),
        edge_relations.reshape(1, edges),
        edge_tails.reshape(1, edges),
        plan,
        negative_start,
    )
    return entity_new.T, state_new.reshape(rows)


def axis_shapes(mesh):
    domains, workers = mesh.shape["dom"], mesh.shape["work"]
    cores = 2 if domains % 2 == 0 else 1
    x_size = max(math.isqrt(workers // 2), 1)
    while workers % x_size:
        x_size -= 1
    return (domains // cores, cores), (workers // x_size, x_size)


def solution(mesh):
    return jax.shard_map(
        functools.partial(body, *axis_shapes(mesh)),
        mesh=mesh,
        in_specs=(
            P(("dom", "work"), None),
            P(("dom", "work")),
            P(),
            P(("dom", "work")),
            P(("dom", "work")),
            P(("dom", "work")),
            P(),
            P(),
        ),
        out_specs=(P(("dom", "work"), None), P(("dom", "work"))),
        check_vma=False,
    )
```

```python
import functools
import math

import jax
import jax.numpy as jnp
from jax import lax
from jax.experimental import pallas as pl
from jax.experimental.pallas import tpu as pltpu
from jax.sharding import PartitionSpec as P

NEG = 1024
learn_rate = 0.1
MESH = pl.DeviceIdType.MESH
F32 = jnp.float32
BF16 = jnp.bfloat16
CODE = jnp.int16


def dot_nn(a, b):
    return lax.dot_general(a, b, (((1,), (0,)), ((), ())), preferred_element_type=F32)


def dot_nt(a, b):
    return lax.dot_general(a, b, (((1,), (1,)), ((), ())), preferred_element_type=F32)


def split(value):
    high = value.astype(BF16)
    low = (value - high.astype(F32)).astype(BF16)
    return high, low


def untranspose_pad(value):
    m, n = value.shape
    pad = -m % 128
    if pad:
        value = jnp.concatenate([value, jnp.zeros((pad, n), value.dtype)], axis=0)
    return jnp.transpose(value)[:, :m]


def encode(value):
    largest = jnp.max(jnp.abs(value), axis=0, keepdims=True)
    exponent = jnp.ceil(jnp.log2(jnp.maximum(largest, 1e-30)) + 0.03)
    exponent = jnp.broadcast_to(exponent, (16, value.shape[1]))
    scale = jnp.exp2(15.0 - exponent)[:1]
    code = jnp.floor(value * scale + 0.5).astype(jnp.int32)
    return code.astype(CODE), exponent.astype(jnp.int32).astype(CODE)


def store_code(ref, slot, value):
    rows = value.shape[0]
    code, exponent = encode(value)
    ref[slot, :rows, :] = code
    ref[slot, rows:, :] = exponent


def load_code(ref, slot):
    whole = ref[slot].astype(jnp.int32).astype(F32)
    rows = whole.shape[0] - 16
    scale = jnp.exp2(whole[rows:] - 15.0)[:1]
    return whole[:rows] * scale


class Exchange:
    def __init__(self, ref, device, a, b, a_size, b_size, sems):
        self.ref, self.device = ref, device
        self.a, self.b, self.a_size, self.b_size = a, b, a_size, b_size
        self.a_send, self.a_recv, self.b_send, self.b_recv = sems

    def slot(self, ka, kb):
        a = lax.rem(self.a + self.a_size - ka, self.a_size)
        b = lax.rem(self.b + self.b_size - kb, self.b_size)
        return a * self.b_size + b

    def peer(self, ka, kb):
        a = lax.rem(self.a + ka, self.a_size)
        b = lax.rem(self.b + kb, self.b_size)
        return self.device(a * self.b_size + b)

    def copy(self, slot, peer, send, recv):
        return pltpu.make_async_remote_copy(
            src_ref=self.ref.at[slot],
            dst_ref=self.ref.at[slot],
            send_sem=send,
            recv_sem=recv,
            device_id=peer,
            device_id_type=MESH,
        )

    def first(self, k, arriving=False):
        slot = self.slot(k, 0) if arriving else self.slot(0, 0)
        return self.copy(slot, self.peer(k, 0), self.a_send.at[k], self.a_recv.at[k])

    def second(self, ka, kb, arriving=False):
        slot = self.slot(ka, kb) if arriving else self.slot(ka, 0)
        at = ka * self.b_size + kb
        return self.copy(slot, self.peer(0, kb), self.b_send.at[at], self.b_recv.at[at])

    def start(self):
        for k in range(1, self.a_size):
            self.first(k).start()
        for kb in range(1, self.b_size):
            self.second(0, kb).start()

    def forward(self, k):
        self.first(k, True).wait_recv()
        for kb in range(1, self.b_size):
            self.second(k, kb).start()

    def collect(self):
        for ka in range(self.a_size):
            for kb in range(1, self.b_size):
                self.second(ka, kb, True).wait_recv()

    def finish(self):
        for k in range(1, self.a_size):
            self.first(k).wait_send()
        for ka in range(self.a_size):
            for kb in range(1, self.b_size):
                self.second(ka, kb).wait_send()


def kernel(
    dom_shape,
    work_shape,
    entity_hbm,
    state_hbm,
    relation_hbm,
    heads_hbm,
    relations_hbm,
    tails_hbm,
    plan_hbm,
    start_hbm,
    entity_out,
    state_out,
    entity_ref,
    state_ref,
    relation_vmem,
    heads_ref,
    relations_ref,
    tails_ref,
    plan_ref,
    start_ref,
    parts,
    target_part,
    partial,
    own_partial,
    negative,
    across,
    along_out,
    along_in,
    returned,
    rel_t,
    tail_rows,
    pulled,
    query_t,
    query_e,
    tail_hi,
    tail_lo,
    load_sem,
    *sems,
):
    features, rows = entity_hbm.shape
    half = features // 2
    edges = heads_hbm.shape[1]
    relations = relation_hbm.shape[1]
    chips, cores = dom_shape
    z_size, x_size = work_shape
    part_rows = rows * z_size * x_size
    dom = lax.axis_index("dom")
    me = lax.axis_index("work")
    y, core = dom // cores, lax.rem(dom, cores)
    z, x = me // x_size, lax.rem(me, x_size)

    pairs = (
        (entity_hbm, entity_ref),
        (heads_hbm, heads_ref),
        (relations_hbm, relations_ref),
        (tails_hbm, tails_ref),
        (plan_hbm, plan_ref),
        (start_hbm, start_ref),
        (state_hbm, state_ref),
        (relation_hbm, relation_vmem),
    )
    loads = [
        pltpu.make_async_copy(source, to, load_sem.at[i]) for i, (source, to) in enumerate(pairs)
    ]
    for load in loads:
        load.start()

    def dom_device(index):
        return (index, me)

    def work_device(index):
        return (dom, index)

    part_exchange = Exchange(parts, dom_device, y, core, chips, cores, sems[0:4])
    target_exchange = Exchange(target_part, work_device, z, x, z_size, x_size, sems[4:8])
    return_exchange = Exchange(returned, dom_device, y, core, chips, cores, sems[8:12])
    across_send, across_recv, along_send, along_recv = sems[12:16]

    def hop(source, way):
        slot = source * x_size + x
        return pltpu.make_async_remote_copy(
            src_ref=target_part.at[slot],
            dst_ref=target_part.at[slot],
            send_sem=sems[4].at[source + (z_size if way < 0 else 0)],
            recv_sem=sems[5].at[source],
            device_id=(dom, jnp.clip(z + way, 0, z_size - 1) * x_size + x),
            device_id_type=MESH,
        )

    def side(source, kb, arriving=False):
        slot = source * x_size + (lax.rem(x + x_size - kb, x_size) if arriving else x)
        at = source * x_size + kb
        return pltpu.make_async_remote_copy(
            src_ref=target_part.at[slot],
            dst_ref=target_part.at[slot],
            send_sem=sems[6].at[at],
            recv_sem=sems[7].at[at],
            device_id=(dom, z * x_size + lax.rem(x + kb, x_size)),
            device_id_type=MESH,
        )

    def chain_start():
        @pl.when(z < z_size - 1)
        def _():
            hop(z, 1).start()

        @pl.when(z > 0)
        def _():
            hop(z, -1).start()

        for kb in range(1, x_size):
            side(z, kb).start()

    def chain_forward(source, way):
        hop(source, way).wait_recv()

        @pl.when((z + way >= 0) & (z + way < z_size))
        def _():
            hop(source, way).start()

        for kb in range(1, x_size):
            side(source, kb).start()

    def chain_finish():
        for source in range(z_size):

            @pl.when((z >= source) & (z < z_size - 1))
            def _():
                hop(source, 1).wait_send()

            @pl.when((z <= source) & (z > 0))
            def _():
                hop(source, -1).wait_send()

            for kb in range(1, x_size):
                side(source, kb).wait_send()

    barrier = pltpu.get_barrier_semaphore()
    for exchange in (part_exchange, target_exchange):
        for k in range(1, exchange.a_size):
            pl.semaphore_signal(
                barrier, inc=1, device_id=exchange.peer(k, 0), device_id_type=MESH
            )
        for k in range(1, exchange.b_size):
            pl.semaphore_signal(
                barrier, inc=1, device_id=exchange.peer(0, k), device_id_type=MESH
            )

    loads[0].wait()
    table_t = entity_ref[...].astype(BF16)
    parts[dom] = table_t
    pl.semaphore_wait(barrier, chips + cores + z_size + x_size - 4)
    part_exchange.start()

    for load in loads[1:]:
        load.wait()
    head_local = heads_ref[...] - me * rows
    head_hot = (
        lax.broadcasted_iota(jnp.int32, (rows, edges), 0) == head_local
    ).astype(F32).astype(BF16)
    head_t = dot_nn(table_t, head_hot)

    rel_t[...] = jnp.zeros_like(rel_t)
    step_rows = 512

    def relation_step(step, carry):
        base = pl.multiple_of(step * step_rows, step_rows)
        row = lax.broadcasted_iota(jnp.int32, (step_rows, edges), 0) + base
        hot = (row == relations_ref[...]).astype(F32).astype(BF16)
        rel_t[...] += dot_nn(relation_vmem[:, pl.ds(base, step_rows)], hot)
        return carry

    steps = relations // step_rows
    for k in range(1, chips + 1):
        lax.fori_loop((k - 1) * steps // chips, k * steps // chips, relation_step, 0)
        if k < chips:
            part_exchange.forward(k)
    part_exchange.collect()
    target_part[me] = parts[plan_ref[dom]]
    chain_start()

    rel_x, rel_y = rel_t[:half], rel_t[half:]
    head_x, head_y = head_t[:half], head_t[half:]
    query = jnp.concatenate(
        [head_x * rel_x - head_y * rel_y, head_x * rel_y + head_y * rel_x], axis=0
    )
    query_bf = query.astype(BF16)
    query_t[...] = query_bf
    query_float = query_bf.astype(F32)
    query_e[...] = untranspose_pad(query_float).astype(BF16)

    width = x_size * rows
    factor = 1.0 / math.sqrt(NEG)
    first_negative = start_ref[dom]

    def tail_hot(block):
        row = lax.broadcasted_iota(jnp.int32, (width, edges), 0) + block * width
        return (row == tails_ref[...]).astype(F32).astype(BF16)

    tail_rows[...] = jnp.zeros_like(tail_rows)
    pulled[...] = jnp.zeros_like(pulled)

    def arrivals(distance):
        @pl.when(z - distance >= 0)
        def _():
            chain_forward(z - distance, 1)

        @pl.when(z + distance < z_size)
        def _():
            chain_forward(z + distance, -1)

    def score_block(block):
        for kb in range(1, x_size):
            side(block, kb, True).wait_recv()
        part = jnp.concatenate(
            [target_part[block * x_size + j] for j in range(x_size)], axis=1
        )
        tail_rows[...] += dot_nn(part, tail_hot(block))
        scores = dot_nn(query_e[...], part)
        weights = jax.nn.sigmoid(scores) * factor
        if part_rows > NEG:
            row = lax.broadcasted_iota(jnp.int32, (1, width), 1) + block * width
            offset = row - first_negative
            offset = jnp.where(offset < 0, offset + part_rows, offset)
            weights = jnp.where(offset < NEG, weights, 0.0)
        weights = weights.astype(BF16)
        pulled[...] += dot_nt(part, weights)
        negative[block] = dot_nn(query_t[...], weights)

    def score_step(distance, carry):
        @pl.when(distance < z_size - 1)
        def _():
            arrivals(distance + 1)

        @pl.when(z - distance >= 0)
        def _():
            score_block(z - distance)

        @pl.when((distance > 0) & (z + distance < z_size))
        def _():
            score_block(z + distance)

        return carry

    lax.fori_loop(0, z_size, score_step, 0)
    tail_t = tail_rows[...]
    positive = jnp.sum(query_float * tail_t, axis=0, keepdims=True)
    positive_weight = jax.nn.sigmoid(positive) - 1.0
    high, low = split(positive_weight * query_float)
    tail_hi[...] = high
    tail_lo[...] = low

    def across_copy(block, j, arriving=False):
        k = lax.rem(j - x + x_size, x_size)
        landing = (lax.rem(x_size - k, x_size) if arriving else k) * z_size + block
        return pltpu.make_async_remote_copy(
            src_ref=partial.at[block * x_size + j],
            dst_ref=across.at[landing],
            send_sem=across_send.at[block * x_size + j],
            recv_sem=across_recv.at[landing],
            device_id=(dom, z * x_size + j),
            device_id_type=MESH,
        )

    def along_copy(k):
        return pltpu.make_async_remote_copy(
            src_ref=along_out.at[k],
            dst_ref=along_in.at[k],
            send_sem=along_send.at[k],
            recv_sem=along_recv.at[k],
            device_id=(dom, lax.rem(z + k, z_size) * x_size + x),
            device_id_type=MESH,
        )

    def send_step(step, carry):
        block = lax.rem(z + step + 1, z_size)
        hot = tail_hot(block)
        grad = negative[block] + dot_nt(tail_hi[...], hot) + dot_nt(tail_lo[...], hot)
        for j in range(x_size):
            piece = grad[:, j * rows : (j + 1) * rows]

            @pl.when(x == j)
            def _():
                own_partial[block] = piece

            @pl.when(x != j)
            def _():
                store_code(partial, block * x_size + j, piece)
                across_copy(block, j).start()

        return carry

    lax.fori_loop(0, z_size, send_step, 0)

    def own_gradient():
        grad_t = positive_weight * tail_rows[...] + pulled[...]
        grad_x, grad_y = grad_t[:half], grad_t[half:]
        rel_x, rel_y = rel_t[:half], rel_t[half:]
        head_grad = jnp.concatenate(
            [grad_x * rel_x + grad_y * rel_y, grad_y * rel_x - grad_x * rel_y], axis=0
        )
        high, low = split(head_grad)
        return dot_nt(high, head_hot) + dot_nt(low, head_hot)

    own_grad = None
    for step in range(1, z_size + 1):
        block = lax.rem(z + step, z_size)
        total = own_partial[block]
        for k in range(1, x_size):
            across_copy(block, lax.rem(x + x_size - k, x_size), True).wait_recv()
            total = total + load_code(across, k * z_size + block)
        if step < z_size:
            store_code(along_out, step, total)
            along_copy(step).start()
        if step == z_size - 1:
            own_grad = own_gradient()
    for k in range(1, z_size):
        along_copy(k).wait_recv()
        total = total + load_code(along_in, k)
    store_code(returned, dom, total)
    return_exchange.start()
    giver = jnp.int32(0)
    for p in range(1, chips * cores):
        giver = jnp.where(plan_ref[p] == dom, jnp.int32(p), giver)
    for k in range(1, chips):
        return_exchange.forward(k)
    return_exchange.collect()
    gradient = own_grad + load_code(returned, giver)
    state_new = state_ref[...] + jnp.sum(gradient * gradient, axis=0, keepdims=True) / features
    state_out[...] = state_new
    entity_out[...] = entity_ref[...] - learn_rate * gradient / jnp.sqrt(state_new)

    part_exchange.finish()
    chain_finish()
    return_exchange.finish()
    for k in range(1, z_size):
        along_copy(k).wait_send()
    for block in range(z_size):
        for k in range(1, x_size):
            across_copy(block, lax.rem(x + k, x_size)).wait_send()


def body(
    dom_shape,
    work_shape,
    entity,
    row_state,
    relation_table,
    edge_heads,
    edge_relations,
    edge_tails,
    plan,
    negative_start,
):
    rows, features = entity.shape
    edges = edge_heads.shape[0]
    chips, cores = dom_shape
    z_size, x_size = work_shape
    domains, workers = chips * cores, z_size * x_size
    vmem = pl.BlockSpec(memory_space=pltpu.VMEM)
    coded = (features + 16, rows)
    counts = (
        [chips, chips, domains, domains]
        + [2 * z_size, z_size, workers, workers]
        + [chips, chips, domains, domains]
        + [workers, workers, z_size, z_size]
    )
    entity_new, state_new = pl.pallas_call(
        functools.partial(kernel, dom_shape, work_shape),
        out_shape=(
            jax.ShapeDtypeStruct((features, rows), F32),
            jax.ShapeDtypeStruct((1, rows), F32),
        ),
        in_specs=[pl.BlockSpec(memory_space=pltpu.HBM)] * 8,
        out_specs=(vmem, vmem),
        scratch_shapes=[
            pltpu.VMEM((features, rows), F32),
            pltpu.VMEM((1, rows), F32),
            pltpu.VMEM(relation_table.shape[::-1], BF16),
            pltpu.VMEM((1, edges), jnp.int32),
            pltpu.VMEM((1, edges), jnp.int32),
            pltpu.VMEM((1, edges), jnp.int32),
            pltpu.SMEM(plan.shape, jnp.int32),
            pltpu.SMEM(negative_start.shape, jnp.int32),
            pltpu.VMEM((domains, features, rows), BF16),
            pltpu.VMEM((workers, features, rows), BF16),
            pltpu.VMEM((workers,) + coded, CODE),
            pltpu.VMEM((z_size, features, rows), F32),
            pltpu.VMEM((z_size, features, x_size * rows), F32),
            pltpu.VMEM((workers,) + coded, CODE),
            pltpu.VMEM((z_size,) + coded, CODE),
            pltpu.VMEM((z_size,) + coded, CODE),
            pltpu.VMEM((domains,) + coded, CODE),
            pltpu.VMEM((features, edges), F32),
            pltpu.VMEM((features, edges), F32),
            pltpu.VMEM((features, edges), F32),
            pltpu.VMEM((features, edges), BF16),
            pltpu.VMEM((edges, features), BF16),
            pltpu.VMEM((features, edges), BF16),
            pltpu.VMEM((features, edges), BF16),
            pltpu.SemaphoreType.DMA((8,)),
        ]
        + [pltpu.SemaphoreType.DMA((count,)) for count in counts],
        compiler_params=pltpu.CompilerParams(
            collective_id=0, has_side_effects=True, vmem_limit_bytes=56 << 20
        ),
    )(
        entity.T,
        row_state.reshape(1, rows),
        relation_table.T,
        edge_heads.reshape(1, edges),
        edge_relations.reshape(1, edges),
        edge_tails.reshape(1, edges),
        plan,
        negative_start,
    )
    return entity_new.T, state_new.reshape(rows)


def axis_shapes(mesh):
    domains, workers = mesh.shape["dom"], mesh.shape["work"]
    cores = 2 if domains % 2 == 0 else 1
    x_size = max(math.isqrt(workers // 2), 1)
    while workers % x_size:
        x_size -= 1
    return (domains // cores, cores), (workers // x_size, x_size)


def solution(mesh):
    return jax.shard_map(
        functools.partial(body, *axis_shapes(mesh)),
        mesh=mesh,
        in_specs=(
            P(("dom", "work"), None),
            P(("dom", "work")),
            P(),
            P(("dom", "work")),
            P(("dom", "work")),
            P(("dom", "work")),
            P(),
            P(),
        ),
        out_specs=(P(("dom", "work"), None), P(("dom", "work"))),
        check_vma=False,
    )
```
